128 devices in a mesh: shard: 64 (over z, y, x_hi, core), tensor: 2 (over x_lo).
Axes of the slice: x: 4 (x_hi: 2, x_lo: 2; x = x_hi * 2 + x_lo), y: 4, z: 4, core: 2. Of those that a mesh axis runs over, the one named last changes fastest.
Arguments:
- grads: float32 [64, 2048, 1024], P(None, 'shard', 'tensor'), may hold values from -16 to 16
- momentum: bfloat16 [64, 2048, 1024], P(None, 'shard', 'tensor'), may hold values from -32 to 32
- counts: int32 [1], replicated, may hold values from 1 to 8
- emb_grad: float32 [8192, 2048], P('shard', 'tensor'), may hold values from -6 to 6
- emb_weight: float32 [8192, 2048], P('shard', 'tensor'), may hold values from -6 to 6
- emb_first: float32 [8192, 2048], P('shard', 'tensor'), may hold values from -2 to 2
- emb_second: float32 [8192, 2048], P('shard', 'tensor'), may hold values from 0.01 to 1
- gain_grad: float32 [65536], P(('shard', 'tensor')), may hold values from -6 to 6
- gain_weight: float32 [65536], P(('shard', 'tensor')), may hold values from 0.5 to 1.5
- gain_first: float32 [65536], P(('shard', 'tensor')), may hold values from -2 to 2
- gain_second: float32 [65536], P(('shard', 'tensor')), may hold values from 0.01 to 1
Outputs:
- new_momentum: bfloat16 [64, 2048, 1024], P(None, 'shard', 'tensor')
- update: float32 [64, 2048, 1024], P(None, 'shard', 'tensor')
- emb_weight_new: float32 [8192, 2048], P('shard', 'tensor')
- emb_first_new: float32 [8192, 2048], P('shard', 'tensor')
- emb_second_new: float32 [8192, 2048], P('shard', 'tensor')
- gain_weight_new: float32 [65536], P(('shard', 'tensor'))
- gain_first_new: float32 [65536], P(('shard', 'tensor'))
- gain_second_new: float32 [65536], P(('shard', 'tensor'))
The draws below stay inside these ranges and needn't reach their ends.
All inputs are finite; a program needn't handle non-finite values.
Results may differ from the reference program's by a relative error of at most 0.012.
The reference program's roundings to bfloat16 on the way count: a program that leaves them out, or rounds other values in their place, can miss the bound.
Values may be sent and summed in bfloat16 or wider, within the bound.
A program may use at most 128 MiB of HBM per device.

```python
import math
import jax
import jax.numpy as jnp
from jax import lax

D = 2048
INNER = 1024
NS_STEPS = 4
NMAT = 64
VROWS = 8192
GAINS = 65536


rank_weights = (1.0, 0.7, 0.5, 0.35)


def column_field(key, factor):
    position = jnp.arange(INNER, dtype=jnp.float32) / max(INNER - 1, 1)
    profile = jnp.exp(position * jnp.log(factor))
    values = 0.6 * jnp.clip(jax.random.normal(key, (NMAT, D, INNER), jnp.float32), -3.0, 3.0)
    return values * profile[None, None, :]


def common_part(key, amplitude):
    anchor = jax.random.fold_in(key, 5)
    left_factor = jnp.clip(jax.random.normal(jax.random.fold_in(anchor, 1), (NMAT, D, 4), jnp.float32), -2.5, 2.5)
    right_factor = jnp.clip(jax.random.normal(jax.random.fold_in(anchor, 2), (NMAT, 4, INNER), jnp.float32), -2.5, 2.5)
    summed = jnp.zeros((NMAT, D, INNER), jnp.float32)
    for number in range(4):
        weight_now = amplitude * rank_weights[number]
        summed = summed + weight_now * left_factor[:, :, number][:, :, None] * right_factor[:, number, :][:, None, :]
    return summed


def shared_field(key, salt):
    bulk = column_field(jax.random.fold_in(key, salt), 4.0)
    amplitude = 1.9
    return jnp.clip(bulk + common_part(key, amplitude), -15.5, 15.5)


def draw_grads(key, part):
    return shared_field(key, 11)


def draw_momentum(key, part):
    return (2.0 * shared_field(key, 23)).astype(jnp.bfloat16)


def shard_levels(own_key, shape, cuts, smallest, high):
    loudness, own = 1.0, jax.random.fold_in(own_key, 6)
    for dim, blocks in cuts:
        steps = jnp.exp(jax.random.uniform(jax.random.fold_in(own, dim), (blocks,), jnp.float32, smallest / len(cuts), high / len(cuts)))
        loudness = loudness * jnp.repeat(steps, shape[dim] // blocks).reshape([-1 if axis == dim else 1 for axis in range(len(shape))])
    return loudness


def gaussian(own_key, shape, deviation, most, pieces=(), held_as=jnp.bfloat16):
    loudness = shard_levels(own_key, shape, pieces, -0.22, 0.18) if pieces else 1.0
    drawn = jax.random.normal(own_key, shape, jnp.float32) * deviation * loudness
    return jnp.minimum(jnp.maximum(drawn, -most), most).astype(held_as)


def setup_inputs(seed: int = 0) -> dict:
    arg_keys = jax.random.split(jax.random.key(seed), 12)
    grads = draw_grads(jax.random.fold_in(arg_keys[11], 71), 0)
    momentum = draw_momentum(jax.random.fold_in(arg_keys[11], 71), 0)
    counts = jax.random.randint(arg_keys[2], (1,), 1, 9).astype(jnp.int32)
    emb_grad = gaussian(arg_keys[3], (VROWS, D), 1.0, 6.0, ((0, 64), (1, 2)), jnp.float32)
    emb_weight = gaussian(arg_keys[4], (VROWS, D), 1.0, 6.0, ((0, 64), (1, 2)), jnp.float32)
    emb_first = gaussian(arg_keys[5], (VROWS, D), 0.3, 2.0, ((0, 64), (1, 2)), jnp.float32)
    emb_second = jnp.clip(jnp.exp(math.log(1.0) - 4.6051702 * jax.random.uniform(arg_keys[6], (VROWS, D), jnp.float32) ** shard_levels(arg_keys[6], (VROWS, D), ((0, 64), (1, 2)), -0.2, 0.2)), 0.01, 1.0)
    gain_grad = gaussian(arg_keys[7], (GAINS,), 1.0, 6.0, ((0, 128),), jnp.float32)
    gain_weight = jnp.clip(1.0 + 0.1 * jax.random.normal(arg_keys[8], (GAINS,), jnp.float32), 0.5, 1.5)
    gain_first = gaussian(arg_keys[9], (GAINS,), 0.3, 2.0, ((0, 128),), jnp.float32)
    gain_second = jnp.clip(jnp.exp(math.log(1.0) - 4.6051702 * jax.random.uniform(arg_keys[10], (GAINS,), jnp.float32) ** shard_levels(arg_keys[10], (GAINS,), ((0, 128),), -0.2, 0.2)), 0.01, 1.0)
    return {"grads": grads, "momentum": momentum, "counts": counts, "emb_grad": emb_grad, "emb_weight": emb_weight, "emb_first": emb_first, "emb_second": emb_second, "gain_grad": gain_grad, "gain_weight": gain_weight, "gain_first": gain_first, "gain_second": gain_second}


linear_coef = 3.4445
cubic_coef = -4.775
quintic_coef = 2.0315
momentum_rate = 0.95
learn_rate = 0.01
decay_weight = 0.1
first_rate = 0.9
second_rate = 0.95
adam_floor = 1e-08
norm_floor = 1e-07

def adamw(grad, weight, first, second, inverse):
    scaled = grad * inverse
    first_new = first_rate * first + (1.0 - first_rate) * scaled
    second_new = second_rate * second + (1.0 - second_rate) * scaled * scaled
    weight_new = weight - learn_rate * (first_new / (jnp.sqrt(second_new) + adam_floor) + decay_weight * weight)
    return (weight_new, first_new, second_new)

def orthogonalize(matrix):
    total = jnp.sqrt(jnp.sum(matrix * matrix))
    iterate = (matrix / (total + norm_floor)).astype(jnp.bfloat16)
    result = jnp.zeros(matrix.shape, jnp.float32)
    for number in range(NS_STEPS):
        gram = jnp.dot(iterate.T, iterate, preferred_element_type=jnp.float32).astype(jnp.bfloat16)
        product = jnp.dot(iterate, gram, preferred_element_type=jnp.float32)
        quintic = jnp.dot(product.astype(jnp.bfloat16), gram, preferred_element_type=jnp.float32)
        mixed = linear_coef * iterate.astype(jnp.float32) + cubic_coef * product + quintic_coef * quintic
        if number + 1 == NS_STEPS:
            result = mixed * math.sqrt(D)
        else:
            iterate = mixed.astype(jnp.bfloat16)
    return result

def reference(grads, momentum, counts, emb_grad, emb_weight, emb_first, emb_second, gain_grad, gain_weight, gain_first, gain_second):
    inverse = 1.0 / counts[0].astype(jnp.float32)
    scaled = grads * inverse
    velocity = momentum_rate * momentum.astype(jnp.float32) + scaled
    advance = scaled + momentum_rate * velocity
    update = lax.map(orthogonalize, advance)
    emb_new = adamw(emb_grad, emb_weight, emb_first, emb_second, inverse)
    gain_new = adamw(gain_grad, gain_weight, gain_first, gain_second, inverse)
    return (velocity.astype(jnp.bfloat16), update, emb_new[0], emb_new[1], emb_new[2], gain_new[0], gain_new[1], gain_new[2])
```

```python
import math

import jax
import jax.numpy as jnp
from jax import lax
from jax.experimental import pallas as pl
from jax.experimental.pallas import tpu as pltpu
from jax.sharding import PartitionSpec as P

D = 2048
NS_STEPS = 4

linear_coef = 3.4445
cubic_coef = -4.775
quintic_coef = 2.0315
momentum_rate = 0.95
learn_rate = 0.01
decay_weight = 0.1
first_rate = 0.9
second_rate = 0.95
adam_floor = 1e-08
norm_floor = 1e-07

MESH = pl.DeviceIdType.MESH
WIDE = 1024
BLOCK = 256
SIDE = WIDE // BLOCK
STARTS = [0, 4, 7, 9]
UPPER = 10


def adamw(grad, weight, first, second, inverse):
    scaled = grad * inverse
    first_new = first_rate * first + (1.0 - first_rate) * scaled
    second_new = second_rate * second + (1.0 - second_rate) * scaled * scaled
    weight_new = weight - learn_rate * (
        first_new / (jnp.sqrt(second_new) + adam_floor) + decay_weight * weight
    )
    return (weight_new, first_new, second_new)


def advance_kernel(counts_ref, grads_ref, momentum_ref, new_ref, out_ref):
    inverse = 1.0 / counts_ref[0].astype(jnp.float32)

    def step(k, carry):
        scaled = grads_ref[k] * inverse
        velocity = momentum_rate * momentum_ref[k].astype(jnp.float32) + scaled
        new_ref[k] = velocity.astype(jnp.bfloat16)
        advance = (scaled + momentum_rate * velocity).astype(jnp.bfloat16)
        out_ref[k // 2, 0, k % 2] = advance[:16]
        out_ref[k // 2, 1, k % 2] = advance[16:]
        return carry

    lax.fori_loop(0, grads_ref.shape[0], step, 0)


def advance(counts, grads, momentum):
    group = 8
    return pl.pallas_call(
        advance_kernel,
        grid=(64 // group,),
        in_specs=[
            pl.BlockSpec(memory_space=pltpu.SMEM),
            pl.BlockSpec((group, 32, 512), lambda i: (i, 0, 0)),
            pl.BlockSpec((group, 32, 512), lambda i: (i, 0, 0)),
        ],
        out_specs=[
            pl.BlockSpec((group, 32, 512), lambda i: (i, 0, 0)),
            pl.BlockSpec((group // 2, 2, 2, 16, 512), lambda i: (i, 0, 0, 0, 0)),
        ],
        out_shape=[
            jax.ShapeDtypeStruct((64, 32, 512), jnp.bfloat16),
            jax.ShapeDtypeStruct((32, 2, 2, 16, 512), jnp.bfloat16),
        ],
    )(counts, grads, momentum)


def place_kernel(in_ref, out_ref):
    def step(k, carry):
        for c in range(2):
            out_ref[k, 16 * c : 16 * c + 16] = in_ref[k // 2, c, k % 2].astype(jnp.float32)
        return carry

    lax.fori_loop(0, out_ref.shape[0], step, 0)


def place(blocks):
    group = 8
    return pl.pallas_call(
        place_kernel,
        grid=(64 // group,),
        in_specs=[pl.BlockSpec((group // 2, 2, 2, 16, 512), lambda i: (i, 0, 0, 0, 0))],
        out_specs=pl.BlockSpec((group, 32, 512), lambda i: (i, 0, 0)),
        out_shape=jax.ShapeDtypeStruct((64, 32, 512), jnp.float32),
    )(blocks)


def orthogonalize_kernel(
    in_ref, out_ref, x, g, p, ours, theirs, total, total_in, send_sem, recv_sem, norm_send, norm_recv
):
    shard, tensor = lax.axis_index("shard"), lax.axis_index("tensor")
    other = (shard + 1 - 2 * (shard % 2), tensor)
    barrier = pltpu.get_barrier_semaphore()
    pl.semaphore_signal(barrier, inc=1, device_id=other, device_id_type=MESH)

    total[...] = jnp.zeros_like(total)

    def take(s, carry):
        rows = pl.ds(pl.multiple_of(s * 16, 16), 16)
        squares = jnp.zeros((8, 128), jnp.float32)
        for t in range(2):
            part = in_ref[s, t]
            x[rows, 512 * t : 512 * t + 512] = part
            wide = part.astype(jnp.float32)
            wide = wide * wide
            for j in range(4):
                cut = wide[:, 128 * j : 128 * j + 128]
                squares = squares + cut[:8] + cut[8:]
        total[...] += squares
        return carry

    lax.fori_loop(0, 64, take, 0)
    pl.semaphore_wait(barrier, 1)

    norm_copy = pltpu.make_async_remote_copy(
        total, total_in, norm_send, norm_recv, device_id=other, device_id_type=MESH
    )
    norm_copy.start()

    def send(slot, i):
        blocks = pl.ds(STARTS[i], SIDE - i)
        return pltpu.make_async_remote_copy(
            ours.at[slot, blocks],
            theirs.at[slot, blocks],
            send_sem.at[slot, i],
            recv_sem.at[slot, i],
            device_id=other,
            device_id_type=MESH,
        )

    def iterate(slot, gram_scale):
        for i in range(SIDE):
            left = x[:, BLOCK * i : BLOCK * i + BLOCK]
            for j in range(i, SIDE):
                block = lax.dot_general(
                    left,
                    x[:, BLOCK * j : BLOCK * j + BLOCK],
                    (((0,), (0,)), ((), ())),
                    preferred_element_type=jnp.float32,
                )
                ours[slot, STARTS[i] + j - i] = block.astype(jnp.bfloat16)
            send(slot, i).start()
        if gram_scale is None:
            norm_copy.wait()
            norm = jnp.sqrt(jnp.sum(total[...] + total_in[...])) + norm_floor
            gram_scale = 1.0 / (norm * norm)
            result_scale = 1.0 / norm
        else:
            result_scale = None
        for j in range(SIDE):
            send(slot, j).wait()
            for k in range(j, SIDE):
                number = STARTS[j] + k - j
                block = ours[slot, number].astype(jnp.float32) + theirs[slot, number].astype(jnp.float32)
                if result_scale is not None:
                    block = block * gram_scale
                g[BLOCK * j : BLOCK * j + BLOCK, BLOCK * k : BLOCK * k + BLOCK] = block.astype(jnp.bfloat16)
                if k > j:
                    g[BLOCK * k : BLOCK * k + BLOCK, BLOCK * j : BLOCK * j + BLOCK] = block.T.astype(
                        jnp.bfloat16
                    )

            def multiply(r, carry):
                rows = pl.ds(pl.multiple_of(r * BLOCK, BLOCK), BLOCK)
                p[rows, BLOCK * j : BLOCK * j + BLOCK] = jnp.dot(
                    x[rows, :], g[:, BLOCK * j : BLOCK * j + BLOCK], preferred_element_type=jnp.float32
                )
                return carry

            lax.fori_loop(0, SIDE, multiply, 0)
        return result_scale

    def combined(rows):
        product = p[rows, :]
        quintic = jnp.dot(product.astype(jnp.bfloat16), g[...], preferred_element_type=jnp.float32)
        return linear_coef * x[rows, :].astype(jnp.float32) + cubic_coef * product + quintic_coef * quintic

    def advance_rows(scale):
        def body(r, carry):
            rows = pl.ds(pl.multiple_of(r * BLOCK, BLOCK), BLOCK)
            mixed = combined(rows)
            if scale is not None:
                mixed = mixed * scale
            x[rows, :] = mixed.astype(jnp.bfloat16)
            return carry

        lax.fori_loop(0, SIDE, body, 0)

    advance_rows(iterate(0, None))

    def middle(n, carry):
        iterate(lax.rem(n, 2), 1.0)
        advance_rows(None)
        return carry

    lax.fori_loop(1, NS_STEPS - 1, middle, 0)

    iterate((NS_STEPS - 1) % 2, 1.0)

    def finish(r, carry):
        rows = pl.ds(pl.multiple_of(r * BLOCK, BLOCK), BLOCK)
        mixed = (combined(rows) * math.sqrt(D)).astype(jnp.bfloat16)
        for s in range(BLOCK // 16):
            for t in range(2):
                out_ref[r * (BLOCK // 16) + s, t] = mixed[16 * s : 16 * s + 16, 512 * t : 512 * t + 512]
        return carry

    lax.fori_loop(0, SIDE, finish, 0)


def orthogonalize(blocks):
    vmem = pl.BlockSpec(memory_space=pltpu.VMEM)
    return pl.pallas_call(
        orthogonalize_kernel,
        out_shape=jax.ShapeDtypeStruct((64, 2, 16, 512), jnp.bfloat16),
        in_specs=[vmem],
        out_specs=vmem,
        scratch_shapes=[
            pltpu.VMEM((WIDE, WIDE), jnp.bfloat16),
            pltpu.VMEM((WIDE, WIDE), jnp.bfloat16),
            pltpu.VMEM((WIDE, WIDE), jnp.float32),
            pltpu.VMEM((2, UPPER, BLOCK, BLOCK), jnp.bfloat16),
            pltpu.VMEM((2, UPPER, BLOCK, BLOCK), jnp.bfloat16),
            pltpu.VMEM((8, 128), jnp.float32),
            pltpu.VMEM((8, 128), jnp.float32),
            pltpu.SemaphoreType.DMA((2, SIDE)),
            pltpu.SemaphoreType.DMA((2, SIDE)),
            pltpu.SemaphoreType.DMA,
            pltpu.SemaphoreType.DMA,
        ],
        compiler_params=pltpu.CompilerParams(
            collective_id=1, has_side_effects=True, vmem_limit_bytes=40 * 2**20
        ),
    )(blocks)


def body(
    grads,
    momentum,
    counts,
    emb_grad,
    emb_weight,
    emb_first,
    emb_second,
    gain_grad,
    gain_weight,
    gain_first,
    gain_second,
):
    inverse = 1.0 / counts[0].astype(jnp.float32)
    new_momentum, blocks = advance(counts, grads, momentum)
    owned = lax.all_to_all(
        blocks.reshape(128, 16, 512), ("shard", "tensor"), split_axis=0, concat_axis=0, tiled=True
    )
    finished = orthogonalize(owned.reshape(64, 2, 16, 512))
    back = lax.all_to_all(
        finished.reshape(128, 16, 512), ("shard", "tensor"), split_axis=0, concat_axis=0, tiled=True
    )
    update = place(back.reshape(32, 2, 2, 16, 512))
    emb_new = adamw(emb_grad, emb_weight, emb_first, emb_second, inverse)
    gain_new = adamw(gain_grad, gain_weight, gain_first, gain_second, inverse)
    return (
        new_momentum,
        update,
        emb_new[0],
        emb_new[1],
        emb_new[2],
        gain_new[0],
        gain_new[1],
        gain_new[2],
    )


def solution(mesh):
    matrix = P(None, "shard", "tensor")
    table = P("shard", "tensor")
    gains = P(("shard", "tensor"))
    return jax.shard_map(
        body,
        mesh=mesh,
        in_specs=(matrix, matrix, P(), table, table, table, table, gains, gains, gains, gains),
        out_specs=(matrix, matrix, table, table, table, gains, gains, gains),
        check_vma=False,
    )
```
